128 devices in a mesh: rep: 8 (over y_hi, z), fsdp: 16 (over y_lo, x, core).
Axes of the slice: x: 4, y: 4 (y_hi: 2, y_lo: 2; y = y_hi * 2 + y_lo), z: 4, core: 2. Of those that a mesh axis runs over, the one named last changes fastest.
Arguments:
- attn_out: bfloat16 [8, 4096, 2560], P('rep', 'fsdp'), may hold values from -6 to 6
- residual: bfloat16 [8, 4096, 5120], P('rep', 'fsdp'), may hold values from -400 to 400
- cotangent: bfloat16 [8, 4096, 5120], P('rep', 'fsdp'), may hold values from -2 to 2
- norm_gain: bfloat16 [5120], P('fsdp'), may hold values from 0.29882812 to 3
- params: float32 [8, 5120, 2560], P('rep', 'fsdp'), may hold values from -1 to 1
- first_moment: float32 [8, 5120, 2560], P('rep', 'fsdp'), may hold values from -3 to 3
- second_moment: float32 [8, 5120, 2560], P('rep', 'fsdp'), may hold values from 0.05 to 2
- step_count: int32 [1], replicated, may hold values from 0 to 63
Outputs:
- params_out: float32 [8, 5120, 2560], P('rep', 'fsdp')
- first_out: float32 [8, 5120, 2560], P('rep', 'fsdp')
- second_out: float32 [8, 5120, 2560], P('rep', 'fsdp')
The draws below stay inside these ranges and needn't reach their ends.
All inputs are finite; a program needn't handle non-finite values.
Results may differ from the reference program's by a relative error of at most 0.007.
Values may be sent and summed in bfloat16 or wider, within the bound.
A program may use at most 192 MiB of HBM per device.

```python
import math
import jax
import jax.numpy as jnp
from jax import lax

D = 5120
HW = 2560
REPS = 8
TOKENS = 4096
N_REP = 8


def shared_base(key):
    base_key = jax.random.fold_in(key, 11)
    return jax.random.truncated_normal(base_key, -4.0, 4.0, (REPS, TOKENS, D))


def draw_residual(key, part):
    base = shared_base(key)
    row_top = math.log(10.0)
    row_scale = jnp.exp(jax.random.uniform(jax.random.fold_in(key, 21), (REPS, TOKENS, 1), minval=0.0, maxval=row_top))
    ramp = jnp.exp(math.log(3.0) * jnp.arange(D, dtype=jnp.float32) / (D - 1))
    col_scale = ramp[None, None, :] * jnp.exp(jax.random.uniform(jax.random.fold_in(key, 22), (1, 1, D), minval=0.0, maxval=math.log(3.0)))
    return (base * row_scale * col_scale).astype(jnp.bfloat16)


def draw_cotangent(key, part):
    base = shared_base(key)
    own_key = jax.random.fold_in(key, 31)
    own = jax.random.truncated_normal(own_key, -4.0, 4.0, (REPS, TOKENS, D))
    return (0.3 * (own + 0.5 * base)).astype(jnp.bfloat16)


def draw_params(key, part):
    scale_value = 1.0 / math.sqrt(HW)
    common_key = jax.random.fold_in(key, 41)
    drift_key = jax.random.fold_in(key, 42)
    common_part = jax.random.truncated_normal(common_key, -4.0, 4.0, (1, D, HW))
    drift_part = jax.random.truncated_normal(drift_key, -4.0, 4.0, (REPS, D, HW))
    return (scale_value * (common_part + 0.01 * drift_part)).astype(jnp.float32)


def shard_levels(rng, extent, cuts, least, largest):
    def one(position, parts):
        steps = jax.random.uniform(jax.random.fold_in(jax.random.fold_in(rng, 6), position), (parts,), jnp.float32, least / len(cuts), largest / len(cuts))
        return jnp.repeat(jnp.exp(steps), extent[position] // parts).reshape((-1,) + (1,) * (len(extent) - position - 1))

    loudness = one(*cuts[0])
    for cut in cuts[1:]:
        loudness = loudness * one(*cut)
    return loudness


def bell_draw(rng, dims, scale, limit, cuts=(), kind=jnp.bfloat16):
    drawn = scale * jax.random.normal(rng, dims, jnp.float32)
    if cuts:
        drawn = drawn * shard_levels(rng, dims, cuts, -0.22, 0.18)
    return jnp.clip(drawn, -limit, limit).astype(kind)


def setup_inputs(seed: int = 0) -> dict:
    key_list = jax.random.split(jax.random.key(seed), 9)
    return {
        "attn_out": bell_draw(key_list[0], (REPS, TOKENS, HW), 1.0, 6.0, ((0, 8), (1, 16))),
        "residual": draw_residual(jax.random.fold_in(key_list[8], 71), 0),
        "cotangent": draw_cotangent(jax.random.fold_in(key_list[8], 71), 0),
        "norm_gain": jnp.clip(jnp.exp(math.log(3.0) - 2.306499 * jax.random.uniform(key_list[3], (D,), jnp.float32) ** shard_levels(key_list[3], (D,), ((0, 16),), -0.2, 0.2)), 0.29882812, 3.0).astype(jnp.bfloat16),
        "params": draw_params(jax.random.fold_in(key_list[8], 71), 0),
        "first_moment": bell_draw(key_list[5], (REPS, D, HW), 0.5, 3.0, ((0, 8), (1, 16)), jnp.float32),
        "second_moment": jnp.clip(jnp.exp(math.log(2.0) - 3.6888794 * jax.random.uniform(key_list[6], (REPS, D, HW), jnp.float32) ** shard_levels(key_list[6], (REPS, D, HW), ((0, 8), (1, 16)), -0.2, 0.2)), 0.05, 2.0),
        "step_count": jax.random.randint(key_list[7], (1,), 0, 64).astype(jnp.int32),
    }


beta_one = 0.9
beta_two = 0.999
learn_rate = 0.001
decay_rate = 0.1
norm_eps = 1e-05
adam_eps = 1e-08

def reference(attn_out, residual, cotangent, norm_gain, params, first_moment, second_moment, step_count):
    step_time = (step_count[0] + 1).astype(jnp.float32)
    first_fix = 1.0 - jnp.power(jnp.float32(beta_one), step_time)
    second_fix = 1.0 - jnp.power(jnp.float32(beta_two), step_time)
    gain_wide = norm_gain.astype(jnp.float32)
    updated_all = []
    first_all = []
    second_all = []
    for replica in range(REPS):
        w_half = params[replica].astype(jnp.bfloat16)
        pre_norm = residual[replica].astype(jnp.float32) + jnp.dot(attn_out[replica], w_half.T, preferred_element_type=jnp.float32)
        scaled = gain_wide[None, :] * cotangent[replica].astype(jnp.float32)
        square_sum = lax.optimization_barrier(jnp.sum(pre_norm * pre_norm, axis=1))
        cross_sum = lax.optimization_barrier(jnp.sum(pre_norm * scaled, axis=1))
        inv_rms = lax.rsqrt(square_sum / D + norm_eps)
        correction = inv_rms * inv_rms * inv_rms * cross_sum / D
        grad_pre = (inv_rms[:, None] * scaled - pre_norm * correction[:, None]).astype(jnp.bfloat16)
        gradient = jnp.dot(grad_pre.T, attn_out[replica], preferred_element_type=jnp.float32)
        first_new = beta_one * first_moment[replica] + (1.0 - beta_one) * gradient
        second_new = beta_two * second_moment[replica] + (1.0 - beta_two) * gradient * gradient
        update_step = -learn_rate * (first_new / first_fix / (jnp.sqrt(second_new / second_fix) + adam_eps) + decay_rate * params[replica])
        updated_all.append(params[replica] + update_step)
        first_all.append(first_new)
        second_all.append(second_new)
    updated = jnp.stack(updated_all)
    level_count = N_REP.bit_length() - 1
    partner_level = jnp.remainder(step_count[0], level_count).astype(jnp.int32)
    partner = jnp.bitwise_xor(jnp.arange(REPS, dtype=jnp.int32), jnp.left_shift(jnp.int32(1), partner_level).astype(jnp.int32))
    params_out = 0.5 * (updated[partner] - params) + 0.5 * (updated - params)
    return (params_out, jnp.stack(first_all), jnp.stack(second_all))
```

```python
import functools

import jax
import jax.numpy as jnp
from jax import lax
from jax.experimental import pallas as pl
from jax.experimental.pallas import tpu as pltpu
from jax.sharding import PartitionSpec as P

beta_one = 0.9
beta_two = 0.999
learn_rate = 0.001
decay_rate = 0.1
norm_eps = 1e-05
adam_eps = 1e-08

MESH = pl.DeviceIdType.MESH
N_X = 4
N_ROW = 2 * N_X
N_PH = 4


def remote(src, dst, send_sem, recv_sem, device):
    return pltpu.make_async_remote_copy(
        src_ref=src,
        dst_ref=dst,
        send_sem=send_sem,
        recv_sem=recv_sem,
        device_id=device,
        device_id_type=MESH,
    )


def step_kernel(
    bit,
    attn, resid, cotan, gain_in, params, first_in, second_in, fixes,
    params_out, first_out, second_out,
    attn_v, res_v, cot_v, w_v, w_s, gain_r, pre_v, gp_v, acc, sums_v, inv_v, cor_v, st_s, st_r,
    gs_v, near_v, far_v, p_v, pf_v, m_v, v_v, us_v, uf_v,
    own_sem, loc_sem, attn_ss, attn_rs, fwd_ss, rel_ss, a2a_ss, a2a_rs, w_ss, w_rs, g_ss, g_rs,
    pf_ss, pf_rs, st_ss, st_rs, far_ss, far_rs, near_ss, near_rs, u_ss, u_rs, out_sem,
):
    tokens = attn.shape[1]
    piece = tokens // N_PH
    half = piece // 2
    pair = N_ROW * piece
    width = resid.shape[2]
    shard = params.shape[1]
    feats = 2 * shard
    n_chunk, _, chunk = acc.shape

    rep = lax.axis_index("rep")
    me = lax.axis_index("fsdp")
    y = lax.div(me, N_ROW)
    idx = lax.rem(me, N_ROW)
    x = lax.div(idx, 2)
    c = lax.rem(idx, 2)
    oc = 1 - c
    oy = 1 - y
    keeper = c == y
    chips = (x, lax.rem(x + 1, N_X), lax.rem(x + N_X - 1, N_X), lax.rem(x + 2, N_X))
    mirror = (0, 2, 1, 3)

    def dev(yy, xx, cc):
        return (rep, yy * N_ROW + xx * 2 + cc)

    m = 1 << bit
    peer = (rep + m * (1 - 2 * lax.rem(lax.div(rep, m), 2)), me)
    right, left, other = dev(y, chips[1], c), dev(y, chips[2], c), dev(y, x, oc)
    row_peers = [(rep, y * N_ROW + lax.rem(idx + k, N_ROW)) for k in range(1, N_ROW)]
    greet = row_peers + [dev(oy, x, 0), dev(oy, x, 1), peer]

    def rows(s, chip, core, part=None):
        start = s * pair + (chip * 2 + core) * piece
        if part is None:
            return pl.ds(pl.multiple_of(start, piece), piece)
        return pl.ds(pl.multiple_of(start + part * half, half), half)

    def cols(chip, core):
        return pl.ds(pl.multiple_of((core * N_X + chip) * feats, feats), feats)

    def own_load(s, which):
        src = pl.ds(s * piece, piece)
        if which == 2:
            return pltpu.make_async_copy(
                attn.at[0, src], attn_v.at[rows(s, x, c)], own_sem.at[s, which]
            )
        source, target = ((resid, res_v), (cotan, cot_v))[which]
        return pltpu.make_async_copy(
            source.at[0, src, cols(x, c)], target.at[rows(s, x, c)], own_sem.at[s, which]
        )

    load_p = pltpu.make_async_copy(params.at[0], p_v, loc_sem.at[0])
    load_m = pltpu.make_async_copy(first_in.at[0], m_v, loc_sem.at[1])
    load_v = pltpu.make_async_copy(second_in.at[0], v_v, loc_sem.at[2])
    load_p.start()

    barrier = pltpu.get_barrier_semaphore()
    for device in greet:
        pl.semaphore_signal(barrier, inc=1, device_id=device, device_id_type=MESH)
    pl.semaphore_wait(barrier, len(greet))

    def tokens_copy(s, order):
        place, device = ((2, right), (1, left), (0, other))[order]
        return remote(
            attn.at[0, pl.ds(s * piece, piece)],
            attn_v.at[rows(s, x, c)],
            attn_ss.at[s, order],
            attn_rs.at[s, place, 0 if place else 1, 0],
            device,
        )

    def features_copy(s, place, rel, which):
        chip, core = chips[mirror[place]], oc if rel else c
        source, target = ((resid, res_v), (cotan, cot_v))[which]
        return remote(
            source.at[0, pl.ds(s * piece, piece), cols(chip, core)],
            target.at[rows(s, x, c)],
            a2a_ss.at[s, place, rel, which],
            a2a_rs.at[s, place, rel, which],
            dev(y, chip, core),
        )

    routes = [
        (place, rel, which)
        for place in (2, 1, 3, 0)
        for rel in range(2)
        for which in range(2)
        if place or rel
    ]

    def send_tokens(s):
        for order in range(3):
            tokens_copy(s, order).start()
        own_load(s, 2).start()

    def send_features(s):
        for route in routes:
            features_copy(s, *route).start()
        own_load(s, 0).start()
        own_load(s, 1).start()

    send_tokens(0)
    send_tokens(1)
    send_features(0)
    pf_copy = remote(params.at[0], pf_v, pf_ss, pf_rs, peer)
    pf_copy.start()

    load_p.wait()
    step = 64 if shard % 64 == 0 else shard

    @pl.loop(0, shard // step)
    def _(i):
        r = pl.ds(pl.multiple_of(i * step, step), step)
        w_s[r, :] = p_v[r, :].astype(jnp.bfloat16)

    own_w = pl.ds(pl.multiple_of(c * shard, shard), shard)
    w_far = remote(w_s, w_v.at[own_w], w_ss.at[0], w_rs.at[c], dev(oy, x, y))
    g_far = remote(gain_in, gain_r.at[c], g_ss.at[0], g_rs.at[c], dev(oy, x, y))
    w_near = remote(w_s, w_v.at[own_w], w_ss.at[1], w_rs.at[c], other)
    g_near = remote(gain_in, gain_r.at[c], g_ss.at[1], g_rs.at[c], other)
    w_far.start()
    g_far.start()

    @pl.when(jnp.logical_not(keeper))
    def _():
        w_near.start()
        g_near.start()

    @pl.when(keeper)
    def _():
        gain_r[c] = gain_in[...]

        @pl.loop(0, shard // step)
        def _(i):
            r = pl.ds(pl.multiple_of(i * step, step), step)
            d = pl.ds(pl.multiple_of(c * shard + i * step, step), step)
            w_v[d, :] = w_s[r, :]

    load_m.start()
    load_v.start()

    @pl.loop(0, n_chunk)
    def _(j):
        acc[j] = jnp.zeros(acc.shape[1:], jnp.float32)

    def arrival(s, place, rel, part=None):
        dst = attn_v.at[rows(s, chips[place], oc if rel else c, part)]
        n = part or 0
        return remote(dst, dst, fwd_ss.at[s, place, n], attn_rs.at[s, place, rel, n], other)

    def forward(s, place, part=None):
        dst = attn_v.at[rows(s, chips[place], c, part)]
        n = part or 0
        return remote(dst, dst, fwd_ss.at[s, place, n], attn_rs.at[s, place, 1, n], other)

    def relay(s, part):
        place, device = ((2, right), (1, left))[part]
        dst = attn_v.at[rows(s, chips[place], c, part)]
        return remote(dst, dst, rel_ss.at[s, part], attn_rs.at[s, 3, 0, part], device)

    def issue(s):
        arrival(s, 2, 0).wait_recv()
        relay(s, 0).start()
        arrival(s, 1, 0).wait_recv()
        relay(s, 1).start()
        forward(s, 1).start()
        forward(s, 2).start()
        if s + 2 < N_PH:
            send_tokens(s + 2)
            send_features(s + 1)
        elif s + 1 == N_PH:
            send_features(s)

    issue(0)

    def w_arrival(core):
        return remote(
            w_s, w_v.at[pl.ds(core * shard, shard)], w_ss.at[0], w_rs.at[core], other
        )

    def g_arrival(core):
        return remote(gain_in, gain_r.at[core], g_ss.at[0], g_rs.at[core], other)

    lane = lax.broadcasted_iota(jnp.int32, (64, 128), 1)

    def st_copy(t, k):
        return remote(
            st_s.at[t], st_r.at[t, k], st_ss.at[t, k], st_rs.at[t, k], row_peers[k - 1]
        )

    def far_copy(j, core):
        return remote(
            gs_v.at[j, pl.ds(core * shard, shard)],
            far_v.at[j],
            far_ss.at[j, core],
            far_rs.at[j],
            dev(oy, x, core),
        )

    def near_copy(j):
        return remote(
            acc.at[j, pl.ds(pl.multiple_of(oc * shard, shard), shard)],
            near_v.at[j],
            near_ss.at[j],
            near_rs.at[j],
            other,
        )

    @pl.loop(0, N_PH)
    def _(t):
        for s in range(N_PH):

            @pl.when(t == s)
            def _():
                if s + 1 < N_PH:
                    issue(s + 1)
                own_load(s, 2).wait()
                arrival(s, 0, 1).wait_recv()
                arrival(s, 1, 1).wait_recv()
                arrival(s, 2, 1).wait_recv()
                for part in range(2):
                    arrival(s, 3, 0, part).wait_recv()
                    forward(s, 3, part).start()
                for part in range(2):
                    arrival(s, 3, 1, part).wait_recv()

        @pl.when(t == 0)
        def _():
            for core in range(2):

                @pl.when(jnp.logical_or(jnp.logical_not(keeper), c != core))
                def _():
                    w_arrival(core).wait_recv()
                    g_arrival(core).wait_recv()

        base = pl.multiple_of(t * pair, pair)
        pre_v[...] = lax.dot_general(
            attn_v[pl.ds(base, pair), :],
            w_v[...],
            (((1,), (1,)), ((), ())),
            preferred_element_type=jnp.float32,
        )

        for s in range(N_PH):

            @pl.when(t == s)
            def _():
                own_load(s, 0).wait()
                own_load(s, 1).wait()
                for place, rel, which in routes:
                    block = (res_v, cot_v)[which].at[rows(s, chips[place], oc if rel else c)]
                    remote(
                        block,
                        block,
                        a2a_ss.at[s, place, rel, which],
                        a2a_rs.at[s, place, rel, which],
                        other,
                    ).wait_recv()

        gain = gain_r[0, 0:1, :] + gain_r[1, 0:1, :]

        @pl.loop(0, pair // 64)
        def _(i):
            r = pl.ds(pl.multiple_of(i * 64, 64), 64)
            b = pl.ds(pl.multiple_of(base + i * 64, 64), 64)
            pre = pre_v[r, :] + res_v[b, :].astype(jnp.float32)
            pre_v[r, :] = pre
            scaled = gain * cot_v[b, :].astype(jnp.float32)
            square = jnp.sum(pre * pre, axis=1, keepdims=True)
            cross = jnp.sum(pre * scaled, axis=1, keepdims=True)
            sums_v[r, :] = jnp.where(lane == 0, square, cross)

        part_sums = sums_v[...].T[0:2, :]
        st_s[t] = part_sums
        for k in range(1, N_ROW):
            st_copy(t, k).start()
        total = part_sums
        for k in range(1, N_ROW):
            st_copy(t, k).wait_recv()
            total = total + st_r[t, k]
        inv_rms = lax.rsqrt(total[0:1, :] / width + norm_eps)
        correction = inv_rms * inv_rms * inv_rms * total[1:2, :] / width
        inv_v[...] = jnp.broadcast_to(inv_rms, (128, pair)).T
        cor_v[...] = jnp.broadcast_to(correction, (128, pair)).T

        sub = min(128, pair)

        @pl.loop(0, pair // sub)
        def _(i):
            r = pl.ds(pl.multiple_of(i * sub, sub), sub)
            b = pl.ds(pl.multiple_of(base + i * sub, sub), sub)
            inv, cor = inv_v[r, :], cor_v[r, :]
            for k in range(feats // 128):
                f = slice(k * 128, (k + 1) * 128)
                scaled = gain[:, f] * cot_v[b, f].astype(jnp.float32)
                grad_pre = (inv * scaled - pre_v[r, f] * cor).astype(jnp.bfloat16)
                gp_v[f, r] = grad_pre.T

        @pl.loop(0, n_chunk)
        def _(j):
            q = pl.ds(pl.multiple_of(j * chunk, chunk), chunk)
            acc[j] += jnp.dot(
                gp_v[...], attn_v[pl.ds(base, pair), q], preferred_element_type=jnp.float32
            )

            @pl.when(jnp.logical_and(t == N_PH - 1, keeper))
            def _():
                near_copy(j).start()

            @pl.when(jnp.logical_and(t == N_PH - 1, jnp.logical_not(keeper)))
            def _():
                gs_v[j] = acc[j].astype(jnp.bfloat16)
                far_copy(j, 0).start()
                far_copy(j, 1).start()

    load_m.wait()
    load_v.wait()
    pf_copy.wait_recv()
    first_fix, second_fix = fixes[0], fixes[1]

    def u_copy(j):
        return remote(us_v.at[j], uf_v.at[j], u_ss.at[j], u_rs.at[j], peer)

    def out_copy(which, src, dst, j):
        q = pl.ds(pl.multiple_of(j * chunk, chunk), chunk)
        return pltpu.make_async_copy(src.at[:, q], dst.at[0, :, q], out_sem.at[which, j])

    def finish(j):
        q = pl.ds(pl.multiple_of(j * chunk, chunk), chunk)
        u_copy(j).wait_recv()

        @pl.loop(0, shard // step)
        def _(i):
            r = pl.ds(pl.multiple_of(i * step, step), step)
            p_v[r, q] = pf_v[r, q] + 0.5 * uf_v[j, r, :].astype(jnp.float32)

        out_copy(0, p_v, params_out, j).start()

    lag = min(2, n_chunk)

    @pl.loop(0, n_chunk)
    def _(j):
        q = pl.ds(pl.multiple_of(j * chunk, chunk), chunk)

        @pl.when(keeper)
        def _():
            near_v[j] = acc[j, pl.ds(pl.multiple_of(c * shard, shard), shard), :]

        @pl.when(jnp.logical_not(keeper))
        def _():
            near_copy(j).wait_recv()

        far_copy(j, 0).wait_recv()

        @pl.loop(0, shard // step)
        def _(i):
            r = pl.ds(pl.multiple_of(i * step, step), step)
            gradient = near_v[j, r, :] + far_v[j, r, :].astype(jnp.float32)
            p = p_v[r, q]
            first_new = beta_one * m_v[r, q] + (1.0 - beta_one) * gradient
            second_new = beta_two * v_v[r, q] + (1.0 - beta_two) * gradient * gradient
            m_v[r, q] = first_new
            v_v[r, q] = second_new
            update = -learn_rate * (
                first_new * first_fix / (jnp.sqrt(second_new * second_fix) + adam_eps)
                + decay_rate * p
            )
            us_v[j, r, :] = update.astype(jnp.bfloat16)
            pf_v[r, q] = 0.5 * (pf_v[r, q] - p) + 0.5 * update

        u_copy(j).start()
        out_copy(1, m_v, first_out, j).start()
        out_copy(2, v_v, second_out, j).start()

        @pl.when(j >= lag)
        def _():
            finish(j - lag)

    @pl.loop(n_chunk - lag, n_chunk)
    def _(j):
        finish(j)

    for s in range(N_PH):
        for order in range(3):
            tokens_copy(s, order).wait_send()
        for route in routes:
            features_copy(s, *route).wait_send()
        for part in range(2):
            relay(s, part).wait_send()
            forward(s, 3, part).wait_send()
        forward(s, 1).wait_send()
        forward(s, 2).wait_send()
    pf_copy.wait_send()
    w_far.wait_send()
    g_far.wait_send()

    @pl.when(jnp.logical_not(keeper))
    def _():
        w_near.wait_send()
        g_near.wait_send()

    @pl.loop(0, N_PH)
    def _(t):
        for k in range(1, N_ROW):
            st_copy(t, k).wait_send()

    @pl.loop(0, n_chunk)
    def _(j):
        @pl.when(keeper)
        def _():
            near_copy(j).wait_send()

        @pl.when(jnp.logical_not(keeper))
        def _():
            far_copy(j, 0).wait_send()
            far_copy(j, 1).wait_send()

        u_copy(j).wait_send()
        out_copy(0, p_v, params_out, j).wait()
        out_copy(1, m_v, first_out, j).wait()
        out_copy(2, v_v, second_out, j).wait()


def run_step(attn, resid, cotan, gain_in, params, first, second, fixes, *, bit):
    tokens, heads = attn.shape[1:]
    shard = params.shape[1]
    feats, row = 2 * shard, N_ROW * tokens
    pair = row // N_PH
    chunk = 256 if heads % 256 == 0 and heads > 256 else 128
    n_chunk = heads // chunk
    bf16, f32, dma = jnp.bfloat16, jnp.float32, pltpu.SemaphoreType.DMA
    any_spec = pl.BlockSpec(memory_space=pl.ANY)
    vmem = pltpu.VMEM
    out = jax.ShapeDtypeStruct(params.shape, f32)
    return pl.pallas_call(
        functools.partial(step_kernel, bit),
        out_shape=(out, out, out),
        in_specs=[
            any_spec,
            any_spec,
            any_spec,
            pl.BlockSpec(memory_space=pltpu.VMEM),
            any_spec,
            any_spec,
            any_spec,
            pl.BlockSpec(memory_space=pltpu.SMEM),
        ],
        out_specs=(any_spec, any_spec, any_spec),
        scratch_shapes=[
            vmem((row, heads), bf16),
            vmem((row, feats), bf16),
            vmem((row, feats), bf16),
            vmem((feats, heads), bf16),
            vmem((shard, heads), bf16),
            vmem((2, 8, feats), f32),
            vmem((pair, feats), f32),
            vmem((feats, pair), bf16),
            vmem((n_chunk, feats, chunk), f32),
            vmem((pair, 128), f32),
            vmem((pair, 128), f32),
            vmem((pair, 128), f32),
            vmem((N_PH, 2, pair), f32),
            vmem((N_PH, N_ROW, 2, pair), f32),
            vmem((n_chunk, feats, chunk), bf16),
            vmem((n_chunk, shard, chunk), f32),
            vmem((n_chunk, shard, chunk), bf16),
            vmem((shard, heads), f32),
            vmem((shard, heads), f32),
            vmem((shard, heads), f32),
            vmem((shard, heads), f32),
            vmem((n_chunk, shard, chunk), bf16),
            vmem((n_chunk, shard, chunk), bf16),
            dma((N_PH, 3)),
            dma((3,)),
            dma((N_PH, 3)),
            dma((N_PH, 4, 2, 2)),
            dma((N_PH, 4, 2)),
            dma((N_PH, 2)),
            dma((N_PH, 4, 2, 2)),
            dma((N_PH, 4, 2, 2)),
            dma((2,)),
            dma((2,)),
            dma((2,)),
            dma((2,)),
            dma,
            dma,
            dma((N_PH, N_ROW)),
            dma((N_PH, N_ROW)),
            dma((n_chunk, 2)),
            dma((n_chunk,)),
            dma((n_chunk,)),
            dma((n_chunk,)),
            dma((n_chunk,)),
            dma((n_chunk,)),
            dma((3, n_chunk)),
        ],
        compiler_params=pltpu.CompilerParams(
            collective_id=bit,
            has_side_effects=True,
            vmem_limit_bytes=63 * 2**20,
        ),
        name=f"step_{bit}",
    )(attn, resid, cotan, gain_in, params, first, second, fixes)


def per_device(attn_out, residual, cotangent, norm_gain, params, first, second, step_count):
    step_time = (step_count[0] + 1).astype(jnp.float32)
    first_fix = 1.0 - jnp.power(jnp.float32(beta_one), step_time)
    second_fix = 1.0 - jnp.power(jnp.float32(beta_two), step_time)
    fixes = jnp.stack([1.0 / first_fix, 1.0 / second_fix])
    shard = norm_gain.shape[0]
    core = lax.rem(lax.axis_index("fsdp"), 2)
    gain = norm_gain.astype(jnp.float32)
    owner = lax.div(lax.broadcasted_iota(jnp.int32, (8, 2 * shard), 1), shard)
    gain_in = jnp.where(owner == core, jnp.concatenate([gain, gain])[None, :], 0.0)
    level_count = lax.axis_size("rep").bit_length() - 1
    level = jnp.remainder(step_count[0], level_count)
    branches = [functools.partial(run_step, bit=bit) for bit in range(level_count)]
    return lax.switch(
        level, branches, attn_out, residual, cotangent, gain_in, params, first, second, fixes
    )


def solution(mesh):
    split = P("rep", "fsdp", None)
    return jax.shard_map(
        per_device,
        mesh=mesh,
        in_specs=(split, split, split, P("fsdp"), split, split, split, P()),
        out_specs=(split, split, split),
        check_vma=False,
    )
```

```python
import functools

import jax
import jax.numpy as jnp
from jax import lax
from jax.experimental import pallas as pl
from jax.experimental.pallas import tpu as pltpu
from jax.sharding import PartitionSpec as P

beta_one = 0.9
beta_two = 0.999
learn_rate = 0.001
decay_rate = 0.1
norm_eps = 1e-05
adam_eps = 1e-08

MESH = pl.DeviceIdType.MESH
N_X = 4
N_ROW = 2 * N_X
N_PH = 4


def remote(src, dst, send_sem, recv_sem, device):
    return pltpu.make_async_remote_copy(
        src_ref=src,
        dst_ref=dst,
        send_sem=send_sem,
        recv_sem=recv_sem,
        device_id=device,
        device_id_type=MESH,
    )


def step_kernel(
    bit,
    attn, resid, cotan, gain_in, params, first_in, second_in, fixes,
    params_out, first_out, second_out,
    attn_v, res_v, cot_v, w_v, w_s, gain_r, pre_v, gp_v, acc, sums_v, inv_v, cor_v, st_s, st_r,
    gs_v, near_v, far_v, p_v, pf_v, m_v, v_v, us_v, uf_v,
    own_sem, loc_sem, attn_ss, attn_rs, fwd_ss, rel_ss, a2a_ss, a2a_rs, w_ss, w_rs, g_ss, g_rs,
    pf_ss, pf_rs, st_ss, st_rs, far_ss, far_rs, near_ss, near_rs, u_ss, u_rs, out_sem,
):
    tokens = attn.shape[1]
    piece = tokens // N_PH
    half = piece // 2
    pair = N_ROW * piece
    width = resid.shape[2]
    shard = params.shape[1]
    feats = 2 * shard
    n_chunk, _, chunk = acc.shape

    rep = lax.axis_index("rep")
    me = lax.axis_index("fsdp")
    y = lax.div(me, N_ROW)
    idx = lax.rem(me, N_ROW)
    x = lax.div(idx, 2)
    c = lax.rem(idx, 2)
    oc = 1 - c
    oy = 1 - y
    keeper = c == y
    chips = (x, lax.rem(x + 1, N_X), lax.rem(x + N_X - 1, N_X), lax.rem(x + 2, N_X))
    mirror = (0, 2, 1, 3)

    def dev(yy, xx, cc):
        return (rep, yy * N_ROW + xx * 2 + cc)

    m = 1 << bit
    peer = (rep + m * (1 - 2 * lax.rem(lax.div(rep, m), 2)), me)
    right, left, other = dev(y, chips[1], c), dev(y, chips[2], c), dev(y, x, oc)
    row_peers = [(rep, y * N_ROW + lax.rem(idx + k, N_ROW)) for k in range(1, N_ROW)]
    greet = row_peers + [dev(oy, x, 0), dev(oy, x, 1), peer]

    def rows(s, chip, core, part=None):
        start = s * pair + (chip * 2 + core) * piece
        if part is None:
            return pl.ds(pl.multiple_of(start, piece), piece)
        return pl.ds(pl.multiple_of(start + part * half, half), half)

    def cols(chip, core):
        return pl.ds(pl.multiple_of((core * N_X + chip) * feats, feats), feats)

    def own_load(s, which):
        src = pl.ds(s * piece, piece)
        if which == 2:
            return pltpu.make_async_copy(
                attn.at[0, src], attn_v.at[rows(s, x, c)], own_sem.at[s, which]
            )
        source, target = ((resid, res_v), (cotan, cot_v))[which]
        return pltpu.make_async_copy(
            source.at[0, src, cols(x, c)], target.at[rows(s, x, c)], own_sem.at[s, which]
        )

    load_p = pltpu.make_async_copy(params.at[0], p_v, loc_sem.at[0])
    load_m = pltpu.make_async_copy(first_in.at[0], m_v, loc_sem.at[1])
    load_v = pltpu.make_async_copy(second_in.at[0], v_v, loc_sem.at[2])
    load_p.start()

    barrier = pltpu.get_barrier_semaphore()
    for device in greet:
        pl.semaphore_signal(barrier, inc=1, device_id=device, device_id_type=MESH)
    pl.semaphore_wait(barrier, len(greet))

    def tokens_copy(s, order):
        place, device = ((2, right), (1, left), (0, other))[order]
        return remote(
            attn.at[0, pl.ds(s * piece, piece)],
            attn_v.at[rows(s, x, c)],
            attn_ss.at[s, order],
            attn_rs.at[s, place, 0 if place else 1, 0],
            device,
        )

    def features_copy(s, place, rel, which):
        chip, core = chips[mirror[place]], oc if rel else c
        source, target = ((resid, res_v), (cotan, cot_v))[which]
        return remote(
            source.at[0, pl.ds(s * piece, piece), cols(chip, core)],
            target.at[rows(s, x, c)],
            a2a_ss.at[s, place, rel, which],
            a2a_rs.at[s, place, rel, which],
            dev(y, chip, core),
        )

    near_routes = [(p, rel, which) for p in (2, 1) for rel in range(2) for which in range(2)]
    near_routes += [(0, 1, 0), (0, 1, 1)]
    far_routes = [(3, rel, which) for rel in range(2) for which in range(2)]

    def send_tokens(s):
        for order in range(3):
            tokens_copy(s, order).start()
        own_load(s, 2).start()

    def send_near_features(s):
        for route in near_routes:
            features_copy(s, *route).start()
        own_load(s, 0).start()
        own_load(s, 1).start()

    def send_far_features(s):
        for route in far_routes:
            features_copy(s, *route).start()

    send_tokens(0)
    send_near_features(0)
    send_far_features(0)
    load_p.wait()
    step = 64 if shard % 64 == 0 else shard

    @pl.loop(0, shard // step)
    def _(i):
        r = pl.ds(pl.multiple_of(i * step, step), step)
        w_s[r, :] = p_v[r, :].astype(jnp.bfloat16)

    own_w = pl.ds(pl.multiple_of(c * shard, shard), shard)
    w_far = remote(w_s, w_v.at[own_w], w_ss.at[0], w_rs.at[c], dev(oy, x, y))
    g_far = remote(gain_in, gain_r.at[c], g_ss.at[0], g_rs.at[c], dev(oy, x, y))
    w_near = remote(w_s, w_v.at[own_w], w_ss.at[1], w_rs.at[c], other)
    g_near = remote(gain_in, gain_r.at[c], g_ss.at[1], g_rs.at[c], other)
    w_far.start()
    g_far.start()

    @pl.when(jnp.logical_not(keeper))
    def _():
        w_near.start()
        g_near.start()

    @pl.when(keeper)
    def _():
        gain_r[c] = gain_in[...]

        @pl.loop(0, shard // step)
        def _(i):
            r = pl.ds(pl.multiple_of(i * step, step), step)
            d = pl.ds(pl.multiple_of(c * shard + i * step, step), step)
            w_v[d, :] = w_s[r, :]

    pf_copy = remote(params.at[0], pf_v, pf_ss, pf_rs, peer)
    pf_copy.start()
    load_m.start()
    load_v.start()

    @pl.loop(0, n_chunk)
    def _(j):
        acc[j] = jnp.zeros(acc.shape[1:], jnp.float32)

    def arrival(s, place, rel, part=None):
        dst = attn_v.at[rows(s, chips[place], oc if rel else c, part)]
        n = part or 0
        return remote(dst, dst, fwd_ss.at[s, place, n], attn_rs.at[s, place, rel, n], other)

    def forward(s, place, part=None):
        dst = attn_v.at[rows(s, chips[place], c, part)]
        n = part or 0
        return remote(dst, dst, fwd_ss.at[s, place, n], attn_rs.at[s, place, 1, n], other)

    def relay(s, part):
        place, device = ((2, right), (1, left))[part]
        dst = attn_v.at[rows(s, chips[place], c, part)]
        return remote(dst, dst, rel_ss.at[s, part], attn_rs.at[s, 3, 0, part], device)

    def pass_on(s):
        arrival(s, 2, 0).wait_recv()
        relay(s, 0).start()
        arrival(s, 1, 0).wait_recv()
        relay(s, 1).start()
        forward(s, 1).start()
        forward(s, 2).start()

    def collect(s):
        own_load(s, 2).wait()
        for part in range(2):
            arrival(s, 3, 0, part).wait_recv()
            forward(s, 3, part).start()
        for place in range(3):
            arrival(s, place, 1).wait_recv()
        for part in range(2):
            arrival(s, 3, 1, part).wait_recv()

    pass_on(0)
    send_tokens(1)
    collect(0)
    send_near_features(1)
    send_far_features(1)
    pass_on(1)

    def w_arrival(core):
        return remote(
            w_s, w_v.at[pl.ds(core * shard, shard)], w_ss.at[0], w_rs.at[core], other
        )

    def g_arrival(core):
        return remote(gain_in, gain_r.at[core], g_ss.at[0], g_rs.at[core], other)

    lane = lax.broadcasted_iota(jnp.int32, (64, 128), 1)

    def st_copy(t, k):
        return remote(
            st_s.at[t], st_r.at[t, k], st_ss.at[t, k], st_rs.at[t, k], row_peers[k - 1]
        )

    def far_copy(j, core):
        return remote(
            gs_v.at[j, pl.ds(core * shard, shard)],
            far_v.at[j],
            far_ss.at[j, core],
            far_rs.at[j],
            dev(oy, x, core),
        )

    def near_copy(j):
        return remote(
            acc.at[j, pl.ds(pl.multiple_of(oc * shard, shard), shard)],
            near_v.at[j],
            near_ss.at[j],
            near_rs.at[j],
            other,
        )

    def matmul_and_sums(t):
        for s in range(1, N_PH):

            @pl.when(t == s)
            def _():
                collect(s)
                if s == 2:
                    send_near_features(3)

        @pl.when(t == 0)
        def _():
            for core in range(2):

                @pl.when(jnp.logical_or(jnp.logical_not(keeper), c != core))
                def _():
                    w_arrival(core).wait_recv()
                    g_arrival(core).wait_recv()

        base = pl.multiple_of(t * pair, pair)
        pre_v[...] = lax.dot_general(
            attn_v[pl.ds(base, pair), :],
            w_v[...],
            (((1,), (1,)), ((), ())),
            preferred_element_type=jnp.float32,
        )

        @pl.when(t == 1)
        def _():
            pass_on(2)

        for s in range(N_PH):

            @pl.when(t == s)
            def _():
                own_load(s, 0).wait()
                own_load(s, 1).wait()
                for place, rel, which in near_routes + far_routes:
                    block = (res_v, cot_v)[which].at[rows(s, chips[place], oc if rel else c)]
                    remote(
                        block,
                        block,
                        a2a_ss.at[s, place, rel, which],
                        a2a_rs.at[s, place, rel, which],
                        other,
                    ).wait_recv()

        gain = gain_r[0, 0:1, :] + gain_r[1, 0:1, :]

        @pl.loop(0, pair // 64)
        def _(i):
            r = pl.ds(pl.multiple_of(i * 64, 64), 64)
            b = pl.ds(pl.multiple_of(base + i * 64, 64), 64)
            pre = pre_v[r, :] + res_v[b, :].astype(jnp.float32)
            pre_v[r, :] = pre
            scaled = gain * cot_v[b, :].astype(jnp.float32)
            square = jnp.sum(pre * pre, axis=1, keepdims=True)
            cross = jnp.sum(pre * scaled, axis=1, keepdims=True)
            sums_v[r, :] = jnp.where(lane == 0, square, cross)

        st_s[t] = sums_v[...].T[0:2, :]
        for k in range(1, N_ROW):
            st_copy(t, k).start()

        @pl.when(t == 0)
        def _():
            send_tokens(2)
            send_near_features(2)

        @pl.when(t == 1)
        def _():
            send_far_features(2)
            send_tokens(3)

        @pl.when(t == 2)
        def _():
            pass_on(3)
            send_far_features(3)

    def gradient_part(t):
        base = pl.multiple_of(t * pair, pair)
        gain = gain_r[0, 0:1, :] + gain_r[1, 0:1, :]
        total = st_s[t]
        for k in range(1, N_ROW):
            st_copy(t, k).wait_recv()
            total = total + st_r[t, k]
        inv_rms = lax.rsqrt(total[0:1, :] / width + norm_eps)
        correction = inv_rms * inv_rms * inv_rms * total[1:2, :] / width
        inv_v[...] = jnp.broadcast_to(inv_rms, (128, pair)).T
        cor_v[...] = jnp.broadcast_to(correction, (128, pair)).T

        sub = min(128, pair)

        @pl.loop(0, pair // sub)
        def _(i):
            r = pl.ds(pl.multiple_of(i * sub, sub), sub)
            b = pl.ds(pl.multiple_of(base + i * sub, sub), sub)
            inv, cor = inv_v[r, :], cor_v[r, :]
            for k in range(feats // 128):
                f = slice(k * 128, (k + 1) * 128)
                scaled = gain[:, f] * cot_v[b, f].astype(jnp.float32)
                grad_pre = (inv * scaled - pre_v[r, f] * cor).astype(jnp.bfloat16)
                gp_v[f, r] = grad_pre.T

        @pl.loop(0, n_chunk)
        def _(j):
            q = pl.ds(pl.multiple_of(j * chunk, chunk), chunk)
            acc[j] += jnp.dot(
                gp_v[...], attn_v[pl.ds(base, pair), q], preferred_element_type=jnp.float32
            )

            @pl.when(jnp.logical_and(t == N_PH - 1, keeper))
            def _():
                near_copy(j).start()

            @pl.when(jnp.logical_and(t == N_PH - 1, jnp.logical_not(keeper)))
            def _():
                gs_v[j] = acc[j].astype(jnp.bfloat16)
                far_copy(j, 0).start()
                far_copy(j, 1).start()

    @pl.loop(0, N_PH + 1)
    def _(t):
        @pl.when(t > 0)
        def _():
            gradient_part(t - 1)

        @pl.when(t < N_PH)
        def _():
            matmul_and_sums(t)

    load_m.wait()
    load_v.wait()
    pf_copy.wait_recv()
    first_fix, second_fix = fixes[0], fixes[1]

    def u_copy(j):
        return remote(us_v.at[j], uf_v.at[j], u_ss.at[j], u_rs.at[j], peer)

    def out_copy(which, src, dst, j):
        q = pl.ds(pl.multiple_of(j * chunk, chunk), chunk)
        return pltpu.make_async_copy(src.at[:, q], dst.at[0, :, q], out_sem.at[which, j])

    def finish(j):
        q = pl.ds(pl.multiple_of(j * chunk, chunk), chunk)
        u_copy(j).wait_recv()

        @pl.loop(0, shard // step)
        def _(i):
            r = pl.ds(pl.multiple_of(i * step, step), step)
            p_v[r, q] = pf_v[r, q] + 0.5 * uf_v[j, r, :].astype(jnp.float32)

        out_copy(0, p_v, params_out, j).start()

    lag = min(2, n_chunk)

    @pl.loop(0, n_chunk)
    def _(j):
        q = pl.ds(pl.multiple_of(j * chunk, chunk), chunk)

        @pl.when(keeper)
        def _():
            near_v[j] = acc[j, pl.ds(pl.multiple_of(c * shard, shard), shard), :]

        @pl.when(jnp.logical_not(keeper))
        def _():
            near_copy(j).wait_recv()

        far_copy(j, 0).wait_recv()

        @pl.loop(0, shard // step)
        def _(i):
            r = pl.ds(pl.multiple_of(i * step, step), step)
            gradient = near_v[j, r, :] + far_v[j, r, :].astype(jnp.float32)
            p = p_v[r, q]
            first_new = beta_one * m_v[r, q] + (1.0 - beta_one) * gradient
            second_new = beta_two * v_v[r, q] + (1.0 - beta_two) * gradient * gradient
            m_v[r, q] = first_new
            v_v[r, q] = second_new
            update = -learn_rate * (
                first_new * first_fix / (jnp.sqrt(second_new * second_fix) + adam_eps)
                + decay_rate * p
            )
            us_v[j, r, :] = update.astype(jnp.bfloat16)
            pf_v[r, q] = 0.5 * (pf_v[r, q] - p) + 0.5 * update

        u_copy(j).start()
        out_copy(1, m_v, first_out, j).start()
        out_copy(2, v_v, second_out, j).start()

        @pl.when(j >= lag)
        def _():
            finish(j - lag)

    @pl.loop(n_chunk - lag, n_chunk)
    def _(j):
        finish(j)

    for s in range(N_PH):
        for order in range(3):
            tokens_copy(s, order).wait_send()
        for route in near_routes + far_routes:
            features_copy(s, *route).wait_send()
        for part in range(2):
            relay(s, part).wait_send()
            forward(s, 3, part).wait_send()
        forward(s, 1).wait_send()
        forward(s, 2).wait_send()
    pf_copy.wait_send()
    w_far.wait_send()
    g_far.wait_send()

    @pl.when(jnp.logical_not(keeper))
    def _():
        w_near.wait_send()
        g_near.wait_send()

    @pl.loop(0, N_PH)
    def _(t):
        for k in range(1, N_ROW):
            st_copy(t, k).wait_send()

    @pl.loop(0, n_chunk)
    def _(j):
        @pl.when(keeper)
        def _():
            near_copy(j).wait_send()

        @pl.when(jnp.logical_not(keeper))
        def _():
            far_copy(j, 0).wait_send()
            far_copy(j, 1).wait_send()

        u_copy(j).wait_send()
        out_copy(0, p_v, params_out, j).wait()
        out_copy(1, m_v, first_out, j).wait()
        out_copy(2, v_v, second_out, j).wait()


def run_step(attn, resid, cotan, gain_in, params, first, second, fixes, *, bit):
    tokens, heads = attn.shape[1:]
    shard = params.shape[1]
    feats, row = 2 * shard, N_ROW * tokens
    pair = row // N_PH
    chunk = 256 if heads % 256 == 0 and heads > 256 else 128
    n_chunk = heads // chunk
    bf16, f32, dma = jnp.bfloat16, jnp.float32, pltpu.SemaphoreType.DMA
    any_spec = pl.BlockSpec(memory_space=pl.ANY)
    vmem = pltpu.VMEM
    out = jax.ShapeDtypeStruct(params.shape, f32)
    return pl.pallas_call(
        functools.partial(step_kernel, bit),
        out_shape=(out, out, out),
        in_specs=[
            any_spec,
            any_spec,
            any_spec,
            pl.BlockSpec(memory_space=pltpu.VMEM),
            any_spec,
            any_spec,
            any_spec,
            pl.BlockSpec(memory_space=pltpu.SMEM),
        ],
        out_specs=(any_spec, any_spec, any_spec),
        scratch_shapes=[
            vmem((row, heads), bf16),
            vmem((row, feats), bf16),
            vmem((row, feats), bf16),
            vmem((feats, heads), bf16),
            vmem((shard, heads), bf16),
            vmem((2, 8, feats), f32),
            vmem((pair, feats), f32),
            vmem((feats, pair), bf16),
            vmem((n_chunk, feats, chunk), f32),
            vmem((pair, 128), f32),
            vmem((pair, 128), f32),
            vmem((pair, 128), f32),
            vmem((N_PH, 2, pair), f32),
            vmem((N_PH, N_ROW, 2, pair), f32),
            vmem((n_chunk, feats, chunk), bf16),
            vmem((n_chunk, shard, chunk), f32),
            vmem((n_chunk, shard, chunk), bf16),
            vmem((shard, heads), f32),
            vmem((shard, heads), f32),
            vmem((shard, heads), f32),
            vmem((shard, heads), f32),
            vmem((n_chunk, shard, chunk), bf16),
            vmem((n_chunk, shard, chunk), bf16),
            dma((N_PH, 3)),
            dma((3,)),
            dma((N_PH, 3)),
            dma((N_PH, 4, 2, 2)),
            dma((N_PH, 4, 2)),
            dma((N_PH, 2)),
            dma((N_PH, 4, 2, 2)),
            dma((N_PH, 4, 2, 2)),
            dma((2,)),
            dma((2,)),
            dma((2,)),
            dma((2,)),
            dma,
            dma,
            dma((N_PH, N_ROW)),
            dma((N_PH, N_ROW)),
            dma((n_chunk, 2)),
            dma((n_chunk,)),
            dma((n_chunk,)),
            dma((n_chunk,)),
            dma((n_chunk,)),
            dma((n_chunk,)),
            dma((3, n_chunk)),
        ],
        compiler_params=pltpu.CompilerParams(
            collective_id=bit,
            has_side_effects=True,
            vmem_limit_bytes=63 * 2**20,
        ),
        name=f"step_{bit}",
    )(attn, resid, cotan, gain_in, params, first, second, fixes)


def per_device(attn_out, residual, cotangent, norm_gain, params, first, second, step_count):
    step_time = (step_count[0] + 1).astype(jnp.float32)
    first_fix = 1.0 - jnp.power(jnp.float32(beta_one), step_time)
    second_fix = 1.0 - jnp.power(jnp.float32(beta_two), step_time)
    fixes = jnp.stack([1.0 / first_fix, 1.0 / second_fix])
    shard = norm_gain.shape[0]
    core = lax.rem(lax.axis_index("fsdp"), 2)
    gain = norm_gain.astype(jnp.float32)
    owner = lax.div(lax.broadcasted_iota(jnp.int32, (8, 2 * shard), 1), shard)
    gain_in = jnp.where(owner == core, jnp.concatenate([gain, gain])[None, :], 0.0)
    level_count = lax.axis_size("rep").bit_length() - 1
    level = jnp.remainder(step_count[0], level_count)
    branches = [functools.partial(run_step, bit=bit) for bit in range(level_count)]
    return lax.switch(
        level, branches, attn_out, residual, cotangent, gain_in, params, first, second, fixes
    )


def solution(mesh):
    split = P("rep", "fsdp", None)
    return jax.shard_map(
        per_device,
        mesh=mesh,
        in_specs=(split, split, split, P("fsdp"), split, split, split, P()),
        out_specs=(split, split, split),
        check_vma=False,
    )
```

```python
import functools

import jax
import jax.numpy as jnp
from jax import lax
from jax.experimental import pallas as pl
from jax.experimental.pallas import tpu as pltpu
from jax.sharding import PartitionSpec as P

beta_one = 0.9
beta_two = 0.999
learn_rate = 0.001
decay_rate = 0.1
norm_eps = 1e-05
adam_eps = 1e-08

MESH = pl.DeviceIdType.MESH
N_X = 4
N_ROW = 2 * N_X
N_PH = 4


def remote(src, dst, send_sem, recv_sem, device):
    return pltpu.make_async_remote_copy(
        src_ref=src,
        dst_ref=dst,
        send_sem=send_sem,
        recv_sem=recv_sem,
        device_id=device,
        device_id_type=MESH,
    )


def step_kernel(
    bit,
    attn, resid, cotan, gain_in, params, first_in, second_in, fixes,
    p_out, first_out, second_out,
    attn_v, res_v, cot_v, w_v, w_s, gain_r, pre_v, gp_v, acc, sums_v, inv_v, cor_v, st_s, st_r,
    gs_v, near_v, far_v, pf_v, m_v, v_v, us_v, uf_v,
    own_sem, loc_sem, attn_ss, attn_rs, fwd_ss, rel_ss, a2a_ss, a2a_rs, w_ss, w_rs, g_ss, g_rs,
    pf_ss, pf_rs, st_ss, st_rs, far_ss, far_rs, near_ss, near_rs, u_ss, u_rs, out_sem,
):
    p_v = p_out.at[0]
    tokens = attn.shape[1]
    piece = tokens // N_PH
    half = piece // 2
    pair = N_ROW * piece
    width = resid.shape[2]
    shard = params.shape[1]
    feats = 2 * shard
    n_chunk, _, chunk = acc.shape
    group = 4 if n_chunk % 4 == 0 else 1

    rep = lax.axis_index("rep")
    me = lax.axis_index("fsdp")
    y = lax.div(me, N_ROW)
    idx = lax.rem(me, N_ROW)
    x = lax.div(idx, 2)
    c = lax.rem(idx, 2)
    oc = 1 - c
    oy = 1 - y
    keeper = c == y
    chips = (x, lax.rem(x + 1, N_X), lax.rem(x + N_X - 1, N_X), lax.rem(x + 2, N_X))
    mirror = (0, 2, 1, 3)

    def dev(yy, xx, cc):
        return (rep, yy * N_ROW + xx * 2 + cc)

    m = 1 << bit
    peer = (rep + m * (1 - 2 * lax.rem(lax.div(rep, m), 2)), me)
    right, left, other = dev(y, chips[1], c), dev(y, chips[2], c), dev(y, x, oc)
    row_peers = [(rep, y * N_ROW + lax.rem(idx + k, N_ROW)) for k in range(1, N_ROW)]
    greet = row_peers + [dev(oy, x, 0), dev(oy, x, 1), peer]

    def rows(s, chip, core, part=None):
        start = s * pair + (chip * 2 + core) * piece
        if part is None:
            return pl.ds(pl.multiple_of(start, piece), piece)
        return pl.ds(pl.multiple_of(start + part * half, half), half)

    def cols(chip, core):
        return pl.ds(pl.multiple_of((core * N_X + chip) * feats, feats), feats)

    def own_load(s, which):
        src = pl.ds(s * piece, piece)
        if which == 2:
            return pltpu.make_async_copy(
                attn.at[0, src], attn_v.at[rows(s, x, c)], own_sem.at[s, which]
            )
        source, target = ((resid, res_v), (cotan, cot_v))[which]
        return pltpu.make_async_copy(
            source.at[0, src, cols(x, c)], target.at[rows(s, x, c)], own_sem.at[s, which]
        )

    load_p = pltpu.make_async_copy(params.at[0], p_v, loc_sem.at[0])
    load_m = pltpu.make_async_copy(first_in.at[0], m_v, loc_sem.at[1])
    load_v = pltpu.make_async_copy(second_in.at[0], v_v, loc_sem.at[2])
    load_p.start()

    barrier = pltpu.get_barrier_semaphore()
    for device in greet:
        pl.semaphore_signal(barrier, inc=1, device_id=device, device_id_type=MESH)
    pl.semaphore_wait(barrier, len(greet))

    def tokens_copy(s, order):
        place, device = ((2, right), (1, left), (0, other))[order]
        return remote(
            attn.at[0, pl.ds(s * piece, piece)],
            attn_v.at[rows(s, x, c)],
            attn_ss.at[s, order],
            attn_rs.at[s, place, 0 if place else 1, 0],
            device,
        )

    def features_copy(s, place, rel, which):
        chip, core = chips[mirror[place]], oc if rel else c
        source, target = ((resid, res_v), (cotan, cot_v))[which]
        return remote(
            source.at[0, pl.ds(s * piece, piece), cols(chip, core)],
            target.at[rows(s, x, c)],
            a2a_ss.at[s, place, rel, which],
            a2a_rs.at[s, place, rel, which],
            dev(y, chip, core),
        )

    near_routes = [(p, rel, which) for p in (2, 1) for rel in range(2) for which in range(2)]
    near_routes += [(0, 1, 0), (0, 1, 1)]
    far_routes = [(3, rel, which) for rel in range(2) for which in range(2)]

    def send_tokens(s):
        for order in range(3):
            tokens_copy(s, order).start()
        own_load(s, 2).start()

    def send_near_features(s):
        for route in near_routes:
            features_copy(s, *route).start()
        own_load(s, 0).start()
        own_load(s, 1).start()

    def send_far_features(s):
        for route in far_routes:
            features_copy(s, *route).start()

    send_tokens(0)
    send_near_features(0)
    send_far_features(0)
    load_p.wait()
    step = 64 if shard % 64 == 0 else shard

    @pl.loop(0, shard // step)
    def _(i):
        r = pl.ds(pl.multiple_of(i * step, step), step)
        w_s[r, :] = p_v[r, :].astype(jnp.bfloat16)

    own_w = pl.ds(pl.multiple_of(c * shard, shard), shard)
    w_far = remote(w_s, w_v.at[own_w], w_ss.at[0], w_rs.at[c], dev(oy, x, y))
    g_far = remote(gain_in, gain_r.at[c], g_ss.at[0], g_rs.at[c], dev(oy, x, y))
    w_near = remote(w_s, w_v.at[own_w], w_ss.at[1], w_rs.at[c], other)
    g_near = remote(gain_in, gain_r.at[c], g_ss.at[1], g_rs.at[c], other)
    w_far.start()
    g_far.start()

    @pl.when(jnp.logical_not(keeper))
    def _():
        w_near.start()
        g_near.start()

    @pl.when(keeper)
    def _():
        gain_r[c] = gain_in[...]

        @pl.loop(0, shard // step)
        def _(i):
            r = pl.ds(pl.multiple_of(i * step, step), step)
            d = pl.ds(pl.multiple_of(c * shard + i * step, step), step)
            w_v[d, :] = w_s[r, :]

    pf_copy = remote(params.at[0], pf_v, pf_ss, pf_rs, peer)
    pf_copy.start()
    load_m.start()
    load_v.start()

    @pl.loop(0, n_chunk)
    def _(j):
        acc[j] = jnp.zeros(acc.shape[1:], jnp.float32)

    def arrival(s, place, rel, part=None):
        dst = attn_v.at[rows(s, chips[place], oc if rel else c, part)]
        n = part or 0
        return remote(dst, dst, fwd_ss.at[s, place, n], attn_rs.at[s, place, rel, n], other)

    def forward(s, place, part=None):
        dst = attn_v.at[rows(s, chips[place], c, part)]
        n = part or 0
        return remote(dst, dst, fwd_ss.at[s, place, n], attn_rs.at[s, place, 1, n], other)

    def relay(s, part):
        place, device = ((2, right), (1, left))[part]
        dst = attn_v.at[rows(s, chips[place], c, part)]
        return remote(dst, dst, rel_ss.at[s, part], attn_rs.at[s, 3, 0, part], device)

    def pass_on(s):
        arrival(s, 2, 0).wait_recv()
        relay(s, 0).start()
        arrival(s, 1, 0).wait_recv()
        relay(s, 1).start()
        forward(s, 1).start()
        forward(s, 2).start()

    def collect(s):
        own_load(s, 2).wait()
        for part in range(2):
            arrival(s, 3, 0, part).wait_recv()
            forward(s, 3, part).start()
        for place in range(3):
            arrival(s, place, 1).wait_recv()
        for part in range(2):
            arrival(s, 3, 1, part).wait_recv()

    pass_on(0)
    send_tokens(1)
    collect(0)
    send_near_features(1)
    send_far_features(1)
    pass_on(1)

    def w_arrival(core):
        return remote(
            w_s, w_v.at[pl.ds(core * shard, shard)], w_ss.at[0], w_rs.at[core], other
        )

    def g_arrival(core):
        return remote(gain_in, gain_r.at[core], g_ss.at[0], g_rs.at[core], other)

    lane = lax.broadcasted_iota(jnp.int32, (64, 128), 1)

    def st_copy(t, k):
        return remote(
            st_s.at[t], st_r.at[t, k], st_ss.at[t, k], st_rs.at[t, k], row_peers[k - 1]
        )

    def far_copy(j, core):
        return remote(
            gs_v.at[j, pl.ds(core * shard, shard)],
            far_v.at[j],
            far_ss.at[j, core],
            far_rs.at[j],
            dev(oy, x, core),
        )

    def near_copy(j):
        return remote(
            acc.at[j, pl.ds(pl.multiple_of(oc * shard, shard), shard)],
            near_v.at[j],
            near_ss.at[j],
            near_rs.at[j],
            other,
        )

    def first_matmul(t):
        for s in range(1, N_PH):

            @pl.when(t == s)
            def _():
                collect(s)
                if s == 2:
                    send_near_features(3)

        @pl.when(t == 0)
        def _():
            for core in range(2):

                @pl.when(jnp.logical_or(jnp.logical_not(keeper), c != core))
                def _():
                    w_arrival(core).wait_recv()
                    g_arrival(core).wait_recv()

        base = pl.multiple_of(t * pair, pair)
        pre_v[lax.rem(t, 2)] = lax.dot_general(
            attn_v[pl.ds(base, pair), :],
            w_v[...],
            (((1,), (1,)), ((), ())),
            preferred_element_type=jnp.float32,
        )

        @pl.when(t == 1)
        def _():
            pass_on(2)

    def row_sums(t):
        slot = lax.rem(t, 2)
        base = pl.multiple_of(t * pair, pair)

        for s in range(N_PH):

            @pl.when(t == s)
            def _():
                own_load(s, 0).wait()
                own_load(s, 1).wait()
                for place, rel, which in near_routes + far_routes:
                    block = (res_v, cot_v)[which].at[rows(s, chips[place], oc if rel else c)]
                    remote(
                        block,
                        block,
                        a2a_ss.at[s, place, rel, which],
                        a2a_rs.at[s, place, rel, which],
                        other,
                    ).wait_recv()

        gain = gain_r[0, 0:1, :] + gain_r[1, 0:1, :]

        @pl.loop(0, pair // 64)
        def _(i):
            r = pl.ds(pl.multiple_of(i * 64, 64), 64)
            b = pl.ds(pl.multiple_of(base + i * 64, 64), 64)
            pre = pre_v[slot, r, :] + res_v[b, :].astype(jnp.float32)
            pre_v[slot, r, :] = pre
            scaled = gain * cot_v[b, :].astype(jnp.float32)
            square = jnp.sum(pre * pre, axis=1, keepdims=True)
            cross = jnp.sum(pre * scaled, axis=1, keepdims=True)
            sums_v[r, :] = jnp.where(lane == 0, square, cross)

        st_s[t] = sums_v[...].T[0:2, :]
        for k in range(1, N_ROW):
            st_copy(t, k).start()

        @pl.when(t == 0)
        def _():
            send_tokens(2)
            send_near_features(2)

        @pl.when(t == 1)
        def _():
            send_far_features(2)
            send_tokens(3)

        @pl.when(t == 2)
        def _():
            pass_on(3)
            send_far_features(3)

    def gradient_part(t):
        slot = lax.rem(t, 2)
        base = pl.multiple_of(t * pair, pair)
        gain = gain_r[0, 0:1, :] + gain_r[1, 0:1, :]
        total = st_s[t]
        for k in range(1, N_ROW):
            st_copy(t, k).wait_recv()
            total = total + st_r[t, k]
        inv_rms = lax.rsqrt(total[0:1, :] / width + norm_eps)
        correction = inv_rms * inv_rms * inv_rms * total[1:2, :] / width
        inv_v[...] = jnp.broadcast_to(inv_rms, (128, pair)).T
        cor_v[...] = jnp.broadcast_to(correction, (128, pair)).T

        sub = min(128, pair)

        @pl.loop(0, pair // sub)
        def _(i):
            r = pl.ds(pl.multiple_of(i * sub, sub), sub)
            b = pl.ds(pl.multiple_of(base + i * sub, sub), sub)
            inv, cor = inv_v[r, :], cor_v[r, :]
            for k in range(feats // 128):
                f = slice(k * 128, (k + 1) * 128)
                scaled = gain[:, f] * cot_v[b, f].astype(jnp.float32)
                grad_pre = (inv * scaled - pre_v[slot, r, f] * cor).astype(jnp.bfloat16)
                gp_v[f, r] = grad_pre.T

        @pl.loop(0, n_chunk // group)
        def _(i):
            q = pl.ds(pl.multiple_of(i * group * chunk, group * chunk), group * chunk)
            product = jnp.dot(
                gp_v[...], attn_v[pl.ds(base, pair), q], preferred_element_type=jnp.float32
            )
            for k in range(group):
                acc[i * group + k] += product[:, k * chunk : (k + 1) * chunk]

            @pl.when(jnp.logical_and(t == N_PH - 1, keeper))
            def _():
                for k in range(group):
                    near_copy(i * group + k).start()

            @pl.when(jnp.logical_and(t == N_PH - 1, jnp.logical_not(keeper)))
            def _():
                for k in range(group):
                    j = i * group + k
                    gs_v[j] = acc[j].astype(jnp.bfloat16)
                    far_copy(j, 0).start()
                    far_copy(j, 1).start()

    @pl.loop(0, N_PH + 1)
    def _(t):
        @pl.when(t < N_PH)
        def _():
            first_matmul(t)

        @pl.when(t > 0)
        def _():
            gradient_part(t - 1)

        @pl.when(t < N_PH)
        def _():
            row_sums(t)

    load_m.wait()
    load_v.wait()
    pf_copy.wait_recv()
    first_fix, second_fix = fixes[0], fixes[1]

    def u_copy(j):
        return remote(us_v.at[j], uf_v.at[j], u_ss.at[j], u_rs.at[j], peer)

    def out_copy(which, j):
        q = pl.ds(pl.multiple_of(j * chunk, chunk), chunk)
        return pltpu.make_async_copy(
            (m_v, v_v)[which].at[:, q],
            (first_out, second_out)[which].at[0, :, q],
            out_sem.at[which, j],
        )

    def finish(j):
        q = pl.ds(pl.multiple_of(j * chunk, chunk), chunk)
        u_copy(j).wait_recv()

        @pl.loop(0, shard // step)
        def _(i):
            r = pl.ds(pl.multiple_of(i * step, step), step)
            p_v[r, q] = pf_v[r, q] + 0.5 * uf_v[j, r, :].astype(jnp.float32)

    lag = min(6, n_chunk)

    @pl.loop(0, n_chunk)
    def _(j):
        q = pl.ds(pl.multiple_of(j * chunk, chunk), chunk)

        @pl.when(keeper)
        def _():
            near_v[j] = acc[j, pl.ds(pl.multiple_of(c * shard, shard), shard), :]

        @pl.when(jnp.logical_not(keeper))
        def _():
            near_copy(j).wait_recv()

        far_copy(j, 0).wait_recv()

        @pl.loop(0, 2)
        def _(i):
            r = pl.ds(pl.multiple_of(i * (shard // 2), shard // 2), shard // 2)
            gradient = near_v[j, r, :] + far_v[j, r, :].astype(jnp.float32)
            p = p_v[r, q]
            first_new = beta_one * m_v[r, q] + (1.0 - beta_one) * gradient
            second_new = beta_two * v_v[r, q] + (1.0 - beta_two) * gradient * gradient
            m_v[r, q] = first_new
            v_v[r, q] = second_new
            update = -learn_rate * (
                first_new * first_fix / (jnp.sqrt(second_new * second_fix) + adam_eps)
                + decay_rate * p
            )
            us_v[j, r, :] = update.astype(jnp.bfloat16)
            pf_v[r, q] = 0.5 * (pf_v[r, q] - p) + 0.5 * update

        u_copy(j).start()
        out_copy(0, j).start()
        out_copy(1, j).start()

        @pl.when(j >= lag)
        def _():
            finish(j - lag)

    @pl.loop(n_chunk - lag, n_chunk)
    def _(j):
        finish(j)

    for s in range(N_PH):
        for order in range(3):
            tokens_copy(s, order).wait_send()
        for route in near_routes + far_routes:
            features_copy(s, *route).wait_send()
        for part in range(2):
            relay(s, part).wait_send()
            forward(s, 3, part).wait_send()
        forward(s, 1).wait_send()
        forward(s, 2).wait_send()
    pf_copy.wait_send()
    w_far.wait_send()
    g_far.wait_send()

    @pl.when(jnp.logical_not(keeper))
    def _():
        w_near.wait_send()
        g_near.wait_send()

    @pl.loop(0, N_PH)
    def _(t):
        for k in range(1, N_ROW):
            st_copy(t, k).wait_send()

    @pl.loop(0, n_chunk)
    def _(j):
        @pl.when(keeper)
        def _():
            near_copy(j).wait_send()

        @pl.when(jnp.logical_not(keeper))
        def _():
            far_copy(j, 0).wait_send()
            far_copy(j, 1).wait_send()

        u_copy(j).wait_send()
        out_copy(0, j).wait()
        out_copy(1, j).wait()


def run_step(attn, resid, cotan, gain_in, params, first, second, fixes, *, bit):
    tokens, heads = attn.shape[1:]
    shard = params.shape[1]
    feats, row = 2 * shard, N_ROW * tokens
    pair = row // N_PH
    chunk = 128
    n_chunk = heads // chunk
    bf16, f32, dma = jnp.bfloat16, jnp.float32, pltpu.SemaphoreType.DMA
    any_spec = pl.BlockSpec(memory_space=pltpu.HBM)
    vmem = pltpu.VMEM
    out = jax.ShapeDtypeStruct(params.shape, f32)
    return pl.pallas_call(
        functools.partial(step_kernel, bit),
        out_shape=(out, out, out),
        in_specs=[
            any_spec,
            any_spec,
            any_spec,
            pl.BlockSpec(memory_space=pltpu.VMEM),
            any_spec,
            any_spec,
            any_spec,
            pl.BlockSpec(memory_space=pltpu.SMEM),
        ],
        out_specs=(pl.BlockSpec(memory_space=pltpu.VMEM), any_spec, any_spec),
        scratch_shapes=[
            vmem((row, heads), bf16),
            vmem((row, feats), bf16),
            vmem((row, feats), bf16),
            vmem((feats, heads), bf16),
            vmem((shard, heads), bf16),
            vmem((2, 8, feats), f32),
            vmem((2, pair, feats), f32),
            vmem((feats, pair), bf16),
            vmem((n_chunk, feats, chunk), f32),
            vmem((pair, 128), f32),
            vmem((pair, 128), f32),
            vmem((pair, 128), f32),
            vmem((N_PH, 2, pair), f32),
            vmem((N_PH, N_ROW, 2, pair), f32),
            vmem((n_chunk, feats, chunk), bf16),
            vmem((n_chunk, shard, chunk), f32),
            vmem((n_chunk, shard, chunk), bf16),
            vmem((shard, heads), f32),
            vmem((shard, heads), f32),
            vmem((shard, heads), f32),
            vmem((n_chunk, shard, chunk), bf16),
            vmem((n_chunk, shard, chunk), bf16),
            dma((N_PH, 3)),
            dma((3,)),
            dma((N_PH, 3)),
            dma((N_PH, 4, 2, 2)),
            dma((N_PH, 4, 2)),
            dma((N_PH, 2)),
            dma((N_PH, 4, 2, 2)),
            dma((N_PH, 4, 2, 2)),
            dma((2,)),
            dma((2,)),
            dma((2,)),
            dma((2,)),
            dma,
            dma,
            dma((N_PH, N_ROW)),
            dma((N_PH, N_ROW)),
            dma((n_chunk, 2)),
            dma((n_chunk,)),
            dma((n_chunk,)),
            dma((n_chunk,)),
            dma((n_chunk,)),
            dma((n_chunk,)),
            dma((2, n_chunk)),
        ],
        compiler_params=pltpu.CompilerParams(
            collective_id=bit,
            has_side_effects=True,
            vmem_limit_bytes=54 * 2**20,
        ),
        name=f"step_{bit}",
    )(attn, resid, cotan, gain_in, params, first, second, fixes)


def per_device(attn_out, residual, cotangent, norm_gain, params, first, second, step_count):
    step_time = (step_count[0] + 1).astype(jnp.float32)
    first_fix = 1.0 - jnp.power(jnp.float32(beta_one), step_time)
    second_fix = 1.0 - jnp.power(jnp.float32(beta_two), step_time)
    fixes = jnp.stack([1.0 / first_fix, 1.0 / second_fix])
    shard = norm_gain.shape[0]
    core = lax.rem(lax.axis_index("fsdp"), 2)
    gain = norm_gain.astype(jnp.float32)
    owner = lax.div(lax.broadcasted_iota(jnp.int32, (8, 2 * shard), 1), shard)
    gain_in = jnp.where(owner == core, jnp.concatenate([gain, gain])[None, :], 0.0)
    level_count = lax.axis_size("rep").bit_length() - 1
    level = jnp.remainder(step_count[0], level_count)
    branches = [functools.partial(run_step, bit=bit) for bit in range(level_count)]
    return lax.switch(
        level, branches, attn_out, residual, cotangent, gain_in, params, first, second, fixes
    )


def solution(mesh):
    split = P("rep", "fsdp", None)
    return jax.shard_map(
        per_device,
        mesh=mesh,
        in_specs=(split, split, split, P("fsdp"), split, split, split, P()),
        out_specs=(split, split, split),
        check_vma=False,
    )
```

```python
import functools

import jax
import jax.numpy as jnp
from jax import lax
from jax.experimental import pallas as pl
from jax.experimental.pallas import tpu as pltpu
from jax.sharding import PartitionSpec as P

beta_one = 0.9
beta_two = 0.999
learn_rate = 0.001
decay_rate = 0.1
norm_eps = 1e-05
adam_eps = 1e-08

MESH = pl.DeviceIdType.MESH
N_X = 4
N_ROW = 2 * N_X
N_PH = 4


def remote(src, dst, send_sem, recv_sem, device):
    return pltpu.make_async_remote_copy(
        src_ref=src,
        dst_ref=dst,
        send_sem=send_sem,
        recv_sem=recv_sem,
        device_id=device,
        device_id_type=MESH,
    )


def step_kernel(
    bit,
    attn, resid, cotan, gain_in, params, first_in, second_in, fixes,
    p_out, first_out, second_out,
    attn_v, res_v, cot_v, w_v, w_s, gain_r, pre_v, gp_v, acc, sums_v, inv_v, cor_v, st_s, st_r,
    gs_v, near_v, far_v, pf_v, m_v, v_v, us_v, uf_v,
    own_sem, loc_sem, attn_ss, attn_rs, fwd_ss, rel_ss, a2a_ss, a2a_rs, w_ss, w_rs, g_ss, g_rs,
    pf_ss, pf_rs, st_ss, st_rs, far_ss, far_rs, near_ss, near_rs, u_ss, u_rs, out_sem,
):
    p_v = p_out.at[0]
    tokens = attn.shape[1]
    piece = tokens // N_PH
    half = piece // 2
    pair = N_ROW * piece
    width = resid.shape[2]
    shard = params.shape[1]
    feats = 2 * shard
    n_chunk, _, chunk = acc.shape
    group = 4 if n_chunk % 4 == 0 else 1

    rep = lax.axis_index("rep")
    me = lax.axis_index("fsdp")
    y = lax.div(me, N_ROW)
    idx = lax.rem(me, N_ROW)
    x = lax.div(idx, 2)
    c = lax.rem(idx, 2)
    oc = 1 - c
    oy = 1 - y
    keeper = c == y
    chips = (x, lax.rem(x + 1, N_X), lax.rem(x + N_X - 1, N_X), lax.rem(x + 2, N_X))
    mirror = (0, 2, 1, 3)

    def dev(yy, xx, cc):
        return (rep, yy * N_ROW + xx * 2 + cc)

    m = 1 << bit
    peer = (rep + m * (1 - 2 * lax.rem(lax.div(rep, m), 2)), me)
    right, left, other = dev(y, chips[1], c), dev(y, chips[2], c), dev(y, x, oc)
    row_peers = [(rep, y * N_ROW + lax.rem(idx + k, N_ROW)) for k in range(1, N_ROW)]
    greet = row_peers + [dev(oy, x, 0), dev(oy, x, 1), peer]

    def rows(s, chip, core, part=None):
        start = s * pair + (chip * 2 + core) * piece
        if part is None:
            return pl.ds(pl.multiple_of(start, piece), piece)
        return pl.ds(pl.multiple_of(start + part * half, half), half)

    def cols(chip, core):
        return pl.ds(pl.multiple_of((core * N_X + chip) * feats, feats), feats)

    def own_load(s, which):
        src = pl.ds(s * piece, piece)
        if which == 2:
            return pltpu.make_async_copy(
                attn.at[0, src], attn_v.at[rows(s, x, c)], own_sem.at[s, which]
            )
        source, target = ((resid, res_v), (cotan, cot_v))[which]
        return pltpu.make_async_copy(
            source.at[0, src, cols(x, c)], target.at[rows(s, x, c)], own_sem.at[s, which]
        )

    load_p = pltpu.make_async_copy(params.at[0], p_v, loc_sem.at[0])
    load_m = pltpu.make_async_copy(first_in.at[0], m_v, loc_sem.at[1])
    load_v = pltpu.make_async_copy(second_in.at[0], v_v, loc_sem.at[2])
    load_p.start()

    barrier = pltpu.get_barrier_semaphore()
    for device in greet:
        pl.semaphore_signal(barrier, inc=1, device_id=device, device_id_type=MESH)
    pl.semaphore_wait(barrier, len(greet))

    def tokens_copy(s, order):
        place, device = ((2, right), (1, left), (0, other))[order]
        return remote(
            attn.at[0, pl.ds(s * piece, piece)],
            attn_v.at[rows(s, x, c)],
            attn_ss.at[s, order],
            attn_rs.at[s, place, 0 if place else 1, 0],
            device,
        )

    def features_copy(s, place, rel, which):
        chip, core = chips[mirror[place]], oc if rel else c
        source, target = ((resid, res_v), (cotan, cot_v))[which]
        return remote(
            source.at[0, pl.ds(s * piece, piece), cols(chip, core)],
            target.at[rows(s, x, c)],
            a2a_ss.at[s, place, rel, which],
            a2a_rs.at[s, place, rel, which],
            dev(y, chip, core),
        )

    near_routes = [(p, rel, which) for p in (2, 1) for rel in range(2) for which in range(2)]
    near_routes += [(0, 1, 0), (0, 1, 1)]
    far_routes = [(3, rel, which) for rel in range(2) for which in range(2)]

    def send_tokens(s):
        for order in range(3):
            tokens_copy(s, order).start()
        own_load(s, 2).start()

    def send_near_features(s, parts=(0, 1)):
        for place, rel, which in near_routes:
            if (which if place else 1) in parts:
                features_copy(s, place, rel, which).start()
        if 1 in parts:
            own_load(s, 0).start()
            own_load(s, 1).start()

    def send_far_features(s):
        for route in far_routes:
            features_copy(s, *route).start()

    send_tokens(0)
    send_near_features(0)
    send_far_features(0)
    load_p.wait()
    step = 64 if shard % 64 == 0 else shard

    @pl.loop(0, shard // step)
    def _(i):
        r = pl.ds(pl.multiple_of(i * step, step), step)
        w_s[r, :] = p_v[r, :].astype(jnp.bfloat16)

    own_w = pl.ds(pl.multiple_of(c * shard, shard), shard)
    w_far = remote(w_s, w_v.at[own_w], w_ss.at[0], w_rs.at[c], dev(oy, x, y))
    g_far = remote(gain_in, gain_r.at[c], g_ss.at[0], g_rs.at[c], dev(oy, x, y))
    w_near = remote(w_s, w_v.at[own_w], w_ss.at[1], w_rs.at[c], other)
    g_near = remote(gain_in, gain_r.at[c], g_ss.at[1], g_rs.at[c], other)
    w_far.start()
    g_far.start()

    @pl.when(jnp.logical_not(keeper))
    def _():
        w_near.start()
        g_near.start()

    @pl.when(keeper)
    def _():
        gain_r[c] = gain_in[...]

        @pl.loop(0, shard // step)
        def _(i):
            r = pl.ds(pl.multiple_of(i * step, step), step)
            d = pl.ds(pl.multiple_of(c * shard + i * step, step), step)
            w_v[d, :] = w_s[r, :]

    pf_copy = remote(params.at[0], pf_v, pf_ss, pf_rs, peer)
    pf_copy.start()
    load_m.start()
    load_v.start()

    @pl.loop(0, n_chunk)
    def _(j):
        acc[j] = jnp.zeros(acc.shape[1:], jnp.float32)

    def arrival(s, place, rel, part=None):
        dst = attn_v.at[rows(s, chips[place], oc if rel else c, part)]
        n = part or 0
        return remote(dst, dst, fwd_ss.at[s, place, n], attn_rs.at[s, place, rel, n], other)

    def forward(s, place, part=None):
        dst = attn_v.at[rows(s, chips[place], c, part)]
        n = part or 0
        return remote(dst, dst, fwd_ss.at[s, place, n], attn_rs.at[s, place, 1, n], other)

    def relay(s, part):
        place, device = ((2, right), (1, left))[part]
        dst = attn_v.at[rows(s, chips[place], c, part)]
        return remote(dst, dst, rel_ss.at[s, part], attn_rs.at[s, 3, 0, part], device)

    def pass_on(s):
        arrival(s, 2, 0).wait_recv()
        relay(s, 0).start()
        arrival(s, 1, 0).wait_recv()
        relay(s, 1).start()
        forward(s, 1).start()
        forward(s, 2).start()

    def collect(s):
        own_load(s, 2).wait()
        for part in range(2):
            arrival(s, 3, 0, part).wait_recv()
            forward(s, 3, part).start()
        for place in range(3):
            arrival(s, place, 1).wait_recv()
        for part in range(2):
            arrival(s, 3, 1, part).wait_recv()

    pass_on(0)
    send_tokens(1)
    collect(0)
    send_near_features(1)
    send_far_features(1)
    pass_on(1)

    def w_arrival(core):
        return remote(
            w_s, w_v.at[pl.ds(core * shard, shard)], w_ss.at[0], w_rs.at[core], other
        )

    def g_arrival(core):
        return remote(gain_in, gain_r.at[core], g_ss.at[0], g_rs.at[core], other)

    lane = lax.broadcasted_iota(jnp.int32, (64, 128), 1)

    def st_copy(t, k):
        return remote(
            st_s.at[t], st_r.at[t, k], st_ss.at[t, k], st_rs.at[t, k], row_peers[k - 1]
        )

    def far_copy(j, core):
        return remote(
            gs_v.at[j, pl.ds(core * shard, shard)],
            far_v.at[j],
            far_ss.at[j, core],
            far_rs.at[j],
            dev(oy, x, core),
        )

    def near_copy(j):
        return remote(
            acc.at[j, pl.ds(pl.multiple_of(oc * shard, shard), shard)],
            near_v.at[j],
            near_ss.at[j],
            near_rs.at[j],
            other,
        )

    def first_matmul(t):
        for s in range(1, N_PH):

            @pl.when(t == s)
            def _():
                collect(s)
                if s == 2:
                    send_near_features(3, (0,))

        @pl.when(t == 0)
        def _():
            for core in range(2):

                @pl.when(jnp.logical_or(jnp.logical_not(keeper), c != core))
                def _():
                    w_arrival(core).wait_recv()
                    g_arrival(core).wait_recv()

        base = pl.multiple_of(t * pair, pair)
        pre_v[lax.rem(t, 2)] = lax.dot_general(
            attn_v[pl.ds(base, pair), :],
            w_v[...],
            (((1,), (1,)), ((), ())),
            preferred_element_type=jnp.float32,
        )

        @pl.when(t == 1)
        def _():
            pass_on(2)

    def row_sums(t):
        slot = lax.rem(t, 2)
        base = pl.multiple_of(t * pair, pair)

        for s in range(N_PH):

            @pl.when(t == s)
            def _():
                own_load(s, 0).wait()
                own_load(s, 1).wait()
                for place, rel, which in near_routes + far_routes:
                    block = (res_v, cot_v)[which].at[rows(s, chips[place], oc if rel else c)]
                    remote(
                        block,
                        block,
                        a2a_ss.at[s, place, rel, which],
                        a2a_rs.at[s, place, rel, which],
                        other,
                    ).wait_recv()

        gain = jnp.concatenate([gain_r[0, 0:1, :], gain_r[1, 0:1, :]], axis=1)

        @pl.loop(0, pair // 64)
        def _(i):
            r = pl.ds(pl.multiple_of(i * 64, 64), 64)
            b = pl.ds(pl.multiple_of(base + i * 64, 64), 64)
            pre = pre_v[slot, r, :] + res_v[b, :].astype(jnp.float32)
            pre_v[slot, r, :] = pre
            scaled = gain * cot_v[b, :].astype(jnp.float32)
            square = jnp.sum(pre * pre, axis=1, keepdims=True)
            cross = jnp.sum(pre * scaled, axis=1, keepdims=True)
            sums_v[r, :] = jnp.where(lane == 0, square, cross)

        st_s[t] = sums_v[...].T[0:2, :]
        for k in range(1, N_ROW):
            st_copy(t, k).start()

        @pl.when(t == 0)
        def _():
            send_tokens(2)
            send_near_features(2)

        @pl.when(t == 1)
        def _():
            send_far_features(2)
            send_tokens(3)

        @pl.when(t == 2)
        def _():
            pass_on(3)
            send_near_features(3, (1,))
            send_far_features(3)

    def gradient_part(t):
        slot = lax.rem(t, 2)
        base = pl.multiple_of(t * pair, pair)
        gain = jnp.concatenate([gain_r[0, 0:1, :], gain_r[1, 0:1, :]], axis=1)
        total = st_s[t]
        for k in range(1, N_ROW):
            st_copy(t, k).wait_recv()
            total = total + st_r[t, k]
        inv_rms = lax.rsqrt(total[0:1, :] / width + norm_eps)
        correction = inv_rms * inv_rms * inv_rms * total[1:2, :] / width
        inv_v[...] = jnp.broadcast_to(inv_rms, (128, pair)).T
        cor_v[...] = jnp.broadcast_to(correction, (128, pair)).T

        sub = min(128, pair)

        @pl.loop(0, pair // sub)
        def _(i):
            r = pl.ds(pl.multiple_of(i * sub, sub), sub)
            b = pl.ds(pl.multiple_of(base + i * sub, sub), sub)
            inv, cor = inv_v[r, :], cor_v[r, :]
            for k in range(feats // 128):
                f = slice(k * 128, (k + 1) * 128)
                scaled = gain[:, f] * cot_v[b, f].astype(jnp.float32)
                grad_pre = (inv * scaled - pre_v[slot, r, f] * cor).astype(jnp.bfloat16)
                gp_v[f, r] = grad_pre.T

        @pl.loop(0, n_chunk // group)
        def _(i):
            q = pl.ds(pl.multiple_of(i * group * chunk, group * chunk), group * chunk)
            product = jnp.dot(
                gp_v[...], attn_v[pl.ds(base, pair), q], preferred_element_type=jnp.float32
            )
            for k in range(group):
                acc[i * group + k] += product[:, k * chunk : (k + 1) * chunk]

            @pl.when(jnp.logical_and(t == N_PH - 1, keeper))
            def _():
                for k in range(group):
                    near_copy(i * group + k).start()

            @pl.when(jnp.logical_and(t == N_PH - 1, jnp.logical_not(keeper)))
            def _():
                for k in range(group):
                    j = i * group + k
                    gs_v[j] = acc[j].astype(jnp.bfloat16)
                    far_copy(j, 0).start()
                    far_copy(j, 1).start()

    @pl.loop(0, N_PH + 1)
    def _(t):
        @pl.when(t < N_PH)
        def _():
            first_matmul(t)

        @pl.when(t > 0)
        def _():
            gradient_part(t - 1)

        @pl.when(t < N_PH)
        def _():
            row_sums(t)

    load_m.wait()
    load_v.wait()
    pf_copy.wait_recv()
    first_fix, second_fix = fixes[0], fixes[1]

    def u_copy(j):
        return remote(us_v.at[j], uf_v.at[j], u_ss.at[j], u_rs.at[j], peer)

    def out_copy(which, j):
        q = pl.ds(pl.multiple_of(j * chunk, chunk), chunk)
        return pltpu.make_async_copy(
            (m_v, v_v)[which].at[:, q],
            (first_out, second_out)[which].at[0, :, q],
            out_sem.at[which, j],
        )

    def finish(j):
        q = pl.ds(pl.multiple_of(j * chunk, chunk), chunk)
        u_copy(j).wait_recv()

        @pl.loop(0, shard // step)
        def _(i):
            r = pl.ds(pl.multiple_of(i * step, step), step)
            p_v[r, q] = pf_v[r, q] + 0.5 * uf_v[j, r, :].astype(jnp.float32)

    lag = min(6, n_chunk)

    @pl.loop(0, n_chunk)
    def _(j):
        q = pl.ds(pl.multiple_of(j * chunk, chunk), chunk)

        @pl.when(keeper)
        def _():
            near_v[j] = acc[j, pl.ds(pl.multiple_of(c * shard, shard), shard), :]

        @pl.when(jnp.logical_not(keeper))
        def _():
            near_copy(j).wait_recv()

        far_copy(j, 0).wait_recv()

        @pl.loop(0, 2)
        def _(i):
            r = pl.ds(pl.multiple_of(i * (shard // 2), shard // 2), shard // 2)
            gradient = near_v[j, r, :] + far_v[j, r, :].astype(jnp.float32)
            p = p_v[r, q]
            first_new = beta_one * m_v[r, q] + (1.0 - beta_one) * gradient
            second_new = beta_two * v_v[r, q] + (1.0 - beta_two) * gradient * gradient
            m_v[r, q] = first_new
            v_v[r, q] = second_new
            update = -learn_rate * (
                first_new * first_fix / (jnp.sqrt(second_new * second_fix) + adam_eps)
                + decay_rate * p
            )
            us_v[j, r, :] = update.astype(jnp.bfloat16)
            pf_v[r, q] = 0.5 * (pf_v[r, q] - p) + 0.5 * update

        u_copy(j).start()
        out_copy(0, j).start()
        out_copy(1, j).start()

        @pl.when(j >= lag)
        def _():
            finish(j - lag)

    @pl.loop(n_chunk - lag, n_chunk)
    def _(j):
        finish(j)

    for s in range(N_PH):
        for order in range(3):
            tokens_copy(s, order).wait_send()
        for route in near_routes + far_routes:
            features_copy(s, *route).wait_send()
        for part in range(2):
            relay(s, part).wait_send()
            forward(s, 3, part).wait_send()
        forward(s, 1).wait_send()
        forward(s, 2).wait_send()
    pf_copy.wait_send()
    w_far.wait_send()
    g_far.wait_send()

    @pl.when(jnp.logical_not(keeper))
    def _():
        w_near.wait_send()
        g_near.wait_send()

    @pl.loop(0, N_PH)
    def _(t):
        for k in range(1, N_ROW):
            st_copy(t, k).wait_send()

    @pl.loop(0, n_chunk)
    def _(j):
        @pl.when(keeper)
        def _():
            near_copy(j).wait_send()

        @pl.when(jnp.logical_not(keeper))
        def _():
            far_copy(j, 0).wait_send()
            far_copy(j, 1).wait_send()

        u_copy(j).wait_send()
        out_copy(0, j).wait()
        out_copy(1, j).wait()


def run_step(attn, resid, cotan, gain_in, params, first, second, fixes, *, bit):
    tokens, heads = attn.shape[1:]
    shard = params.shape[1]
    feats, row = 2 * shard, N_ROW * tokens
    pair = row // N_PH
    chunk = 128
    n_chunk = heads // chunk
    bf16, f32, dma = jnp.bfloat16, jnp.float32, pltpu.SemaphoreType.DMA
    any_spec = pl.BlockSpec(memory_space=pltpu.HBM)
    vmem = pltpu.VMEM
    out = jax.ShapeDtypeStruct(params.shape, f32)
    return pl.pallas_call(
        functools.partial(step_kernel, bit),
        out_shape=(out, out, out),
        in_specs=[
            any_spec,
            any_spec,
            any_spec,
            pl.BlockSpec(memory_space=pltpu.VMEM),
            any_spec,
            any_spec,
            any_spec,
            pl.BlockSpec(memory_space=pltpu.SMEM),
        ],
        out_specs=(pl.BlockSpec(memory_space=pltpu.VMEM), any_spec, any_spec),
        scratch_shapes=[
            vmem((row, heads), bf16),
            vmem((row, feats), bf16),
            vmem((row, feats), bf16),
            vmem((feats, heads), bf16),
            vmem((shard, heads), bf16),
            vmem((2, 8, shard), f32),
            vmem((2, pair, feats), f32),
            vmem((feats, pair), bf16),
            vmem((n_chunk, feats, chunk), f32),
            vmem((pair, 128), f32),
            vmem((pair, 128), f32),
            vmem((pair, 128), f32),
            vmem((N_PH, 2, pair), f32),
            vmem((N_PH, N_ROW, 2, pair), f32),
            vmem((n_chunk, feats, chunk), bf16),
            vmem((n_chunk, shard, chunk), f32),
            vmem((n_chunk, shard, chunk), bf16),
            vmem((shard, heads), f32),
            vmem((shard, heads), f32),
            vmem((shard, heads), f32),
            vmem((n_chunk, shard, chunk), bf16),
            vmem((n_chunk, shard, chunk), bf16),
            dma((N_PH, 3)),
            dma((3,)),
            dma((N_PH, 3)),
            dma((N_PH, 4, 2, 2)),
            dma((N_PH, 4, 2)),
            dma((N_PH, 2)),
            dma((N_PH, 4, 2, 2)),
            dma((N_PH, 4, 2, 2)),
            dma((2,)),
            dma((2,)),
            dma((2,)),
            dma((2,)),
            dma,
            dma,
            dma((N_PH, N_ROW)),
            dma((N_PH, N_ROW)),
            dma((n_chunk, 2)),
            dma((n_chunk,)),
            dma((n_chunk,)),
            dma((n_chunk,)),
            dma((n_chunk,)),
            dma((n_chunk,)),
            dma((2, n_chunk)),
        ],
        compiler_params=pltpu.CompilerParams(
            collective_id=bit,
            has_side_effects=True,
            vmem_limit_bytes=54 * 2**20,
        ),
        name=f"step_{bit}",
    )(attn, resid, cotan, gain_in, params, first, second, fixes)


def per_device(attn_out, residual, cotangent, norm_gain, params, first, second, step_count):
    step_time = (step_count[0] + 1).astype(jnp.float32)
    first_fix = 1.0 - jnp.power(jnp.float32(beta_one), step_time)
    second_fix = 1.0 - jnp.power(jnp.float32(beta_two), step_time)
    fixes = jnp.stack([1.0 / first_fix, 1.0 / second_fix])
    gain_in = jnp.broadcast_to(norm_gain.astype(jnp.float32)[None, :], (8, norm_gain.shape[0]))
    level_count = lax.axis_size("rep").bit_length() - 1
    level = jnp.remainder(step_count[0], level_count)
    branches = [functools.partial(run_step, bit=bit) for bit in range(level_count)]
    return lax.switch(
        level, branches, attn_out, residual, cotangent, gain_in, params, first, second, fixes
    )


def solution(mesh):
    split = P("rep", "fsdp", None)
    return jax.shard_map(
        per_device,
        mesh=mesh,
        in_specs=(split, split, split, P("fsdp"), split, split, split, P()),
        out_specs=(split, split, split),
        check_vma=False,
    )
```
